32 devices in a mesh: row: 8 (over z, y), col: 4 (over x, core).
Axes of the slice: x: 2, y: 2, z: 4, core: 2. Of those that a mesh axis runs over, the one named last changes fastest.
Arguments:
- sequence: bfloat16 [128, 1024], P('row'), may hold values from -6 to 6
- pair_state: bfloat16 [128, 128, 128], P('row', 'col'), may hold values from -6 to 6
- residue_mask: int32 [128], replicated, may hold values 0 or 1
- chain_index: int32 [128], replicated, may hold values from 0 to 3, never falling along the last dimension, each value on 1 to 64 neighbouring positions
- attention_in: bfloat16 [1024, 4, 1024], P(None, None, 'col'), may hold values from -0.1875 to 0.1875
- attention_out: bfloat16 [1024, 1024], P('col'), may hold values from -0.1875 to 0.1875
- bias_weight: bfloat16 [128, 32], replicated, may hold values from -40 to 40
- chain_bias: float32 [32], replicated, may hold values from -2 to 2
- outer_in: bfloat16 [1024, 128], replicated, may hold values from -0.1875 to 0.1875
- outer_out: bfloat16 [128, 128], replicated, may hold values from -0.5 to 0.5
- triangle_in: bfloat16 [128, 5, 128], replicated, may hold values from -0.5 to 0.5
- triangle_out: bfloat16 [128, 128], replicated, may hold values from -0.5 to 0.5
- transition_up: bfloat16 [128, 512], replicated, may hold values from -0.5 to 0.5
- transition_down: bfloat16 [512, 128], replicated, may hold values from -0.25 to 0.25
Outputs:
- sequence_out: bfloat16 [128, 1024], P('row')
- pair_out: bfloat16 [128, 128, 128], P('row', 'col')
The draws below stay inside these ranges and needn't reach their ends.
Inputs may be any that keep to these rules, and one draw needn't show every extreme that they name: chain_index never falls along the residues; each chain holds at most 64 residues.
All inputs are finite; a program needn't handle non-finite values.
Results may differ from the reference program's by a relative error of at most 0.0095.
The reference program's roundings to bfloat16 on the way count: a program that leaves them out, or rounds other values in their place, can miss the bound.
Values may be sent and summed in bfloat16 or wider, within the bound.
A program may use at most 64 MiB of HBM per device.

```python
import math
import jax
import jax.numpy as jnp
import numpy as np
from jax import lax

D = 1024
HEADS = 32
HEADDIM = 32
C = 128
P_SIZE = 64
F = 512
L = 128


def draw_bias_weight(key, part):
    base = jax.random.normal(jax.random.fold_in(key, 11), (C, HEADS), jnp.float32)
    values = base * (1.5 / math.sqrt(C))
    return jnp.clip(values, -40.0, 40.0).astype(jnp.bfloat16)


def plant(entries, stream_key, smallest, top_value):
    longest = entries.shape.index(max(entries.shape))
    spots = []
    for shift in (0, 1):
        where = [jax.random.randint(jax.random.fold_in(stream_key, axis), (), 0, length) for axis, length in enumerate(entries.shape)]
        where[longest] = (where[longest] + shift) % entries.shape[longest]
        spots.append(tuple(where))
    return entries.at[spots[0]].set(smallest).at[spots[1]].set(top_value)


def block_levels(own_key, shape, split, smallest, top_value):
    loudness = 1.0
    for dim, shards_of in split:
        draws = jax.random.uniform(jax.random.fold_in(jax.random.fold_in(own_key, 6), dim), (shards_of,), jnp.float32, smallest / len(split), top_value / len(split))
        loudness = loudness * jnp.repeat(jnp.exp(draws), shape[dim] // shards_of).reshape((-1,) + (1,) * (len(shape) - 1 - dim))
    return loudness


def length_profile(number_of, total, limit, skew):
    weights = [(1 << 20) // math.isqrt(standing ** skew) + 1 for standing in range(2, number_of + 1)]
    surplus, holding = total - limit - (number_of - 1), [1] * (number_of - 1)
    while surplus > 0:
        free = [i for i in range(number_of - 1) if holding[i] < limit]
        mass, left = sum([weights[i] for i in free]), surplus
        for i in free:
            more = min(limit - holding[i], max(1, left * weights[i] // mass), surplus)
            holding[i] = holding[i] + more
            surplus = surplus - more
    return np.array([limit] + holding)


def uneven_parts(key, count, total, limit, lean):
    if count == 2:
        one = jax.random.randint(key, (), max(1, total - limit), min(limit, total - 1) + 1)
        return jnp.stack([one, total - one])
    lengths = jnp.asarray(length_profile(count, total, limit, lean), jnp.int32)
    pairs = (count - 1) // 2
    source_of, taker = lengths[1:1 + 2 * pairs:2], lengths[2:2 + 2 * pairs:2]
    room = jnp.minimum(source_of - 1, limit - taker)
    passed = jax.random.randint(jax.random.fold_in(key, 1), (pairs,), 0, 1 << 20) % (room + 1)
    lengths = lengths.at[1:1 + 2 * pairs:2].set(source_of - passed).at[2:2 + 2 * pairs:2].set(taker + passed)
    return lengths[jax.random.permutation(jax.random.fold_in(key, 2), count)]


def gaussian(own_key, shape, width, reach, shards=(), held_as=jnp.bfloat16):
    factor_of = block_levels(own_key, shape, shards, -0.22, 0.18) if shards else 1.0
    drawn = jax.random.normal(own_key, shape, jnp.float32) * width * factor_of
    return jnp.minimum(jnp.maximum(drawn, -reach), reach).astype(held_as)


def setup_inputs(seed: int = 0) -> dict:
    seeds = jax.random.split(jax.random.key(seed), 15)
    sequence = gaussian(seeds[0], (L, D), 1.0, 6.0, ((0, 8),))
    pair_state = gaussian(seeds[1], (L, L, C), 1.0, 6.0, ((0, 8), (1, 4)))
    residue_mask = plant((jax.random.randint(seeds[2], (L,), 0, 8) < 7).astype(jnp.int32), jax.random.fold_in(seeds[2], 1), 0, 1)
    chain_index = jnp.searchsorted(jnp.cumsum(uneven_parts(seeds[3], 4, L, L // 2, 0)), jnp.arange(L), side="right").astype(jnp.int32)
    attention_in = gaussian(seeds[4], (D, 4, D), D ** -0.5, 0.1875, ((2, 4),))
    attention_out = gaussian(seeds[5], (D, D), D ** -0.5, 0.1875, ((0, 4),))
    bias_weight = draw_bias_weight(jax.random.fold_in(seeds[14], 71), 0)
    chain_bias = jnp.clip(jax.random.uniform(seeds[7], (HEADS,), jnp.float32, -2.0, 2.0), -2.0, 2.0)
    outer_in = gaussian(seeds[8], (D, 2 * P_SIZE), D ** -0.5, 0.1875)
    outer_out = gaussian(seeds[9], (2 * P_SIZE, C), (2 * P_SIZE) ** -0.5, 0.5)
    triangle_in = gaussian(seeds[10], (C, 5, C), C ** -0.5, 0.5)
    triangle_out = gaussian(seeds[11], (C, C), C ** -0.5, 0.5)
    transition_up = gaussian(seeds[12], (C, F), C ** -0.5, 0.5)
    transition_down = gaussian(seeds[13], (F, C), F ** -0.5, 0.25)
    return dict(sequence=sequence, pair_state=pair_state, residue_mask=residue_mask, chain_index=chain_index, attention_in=attention_in, attention_out=attention_out, bias_weight=bias_weight, chain_bias=chain_bias, outer_in=outer_in, outer_out=outer_out, triangle_in=triangle_in, triangle_out=triangle_out, transition_up=transition_up, transition_down=transition_down)


def layer_norm(values):
    center = values - lax.optimization_barrier(jnp.mean(values, axis=-1, keepdims=True))
    spread = lax.optimization_barrier(jnp.mean(center * center, axis=-1, keepdims=True))
    return center * lax.rsqrt(spread + 1e-05)

def reference(sequence, pair_state, residue_mask, chain_index, attention_in, attention_out, bias_weight, chain_bias, outer_in, outer_out, triangle_in, triangle_out, transition_up, transition_down):
    pair_wide = pair_state.astype(jnp.float32)
    normed_pair = layer_norm(pair_wide).astype(jnp.bfloat16)
    pair_bias = jnp.einsum('ijc,ch->hij', normed_pair.astype(jnp.float32), bias_weight.astype(jnp.float32))
    normed_seq = layer_norm(sequence.astype(jnp.float32)).astype(jnp.bfloat16)
    projected = jnp.einsum('id,dpe->ipe', normed_seq.astype(jnp.float32), attention_in.astype(jnp.float32))
    query = projected[:, 0].astype(jnp.bfloat16).reshape(L, HEADS, HEADDIM)
    keys = projected[:, 1].astype(jnp.bfloat16).reshape(L, HEADS, HEADDIM)
    values = projected[:, 2].astype(jnp.bfloat16).reshape(L, HEADS, HEADDIM)
    gate = jax.nn.sigmoid(projected[:, 3])
    scale = 1.0 / math.sqrt(HEADDIM)
    scores = jnp.einsum('ihd,jhd->hij', query.astype(jnp.float32), keys.astype(jnp.float32)) * scale
    same_chain = (chain_index[:, None] == chain_index[None, :]).astype(jnp.float32)
    scores = scores + pair_bias + chain_bias[:, None, None] * same_chain[None]
    positions = jnp.arange(L, dtype=jnp.int32)
    allowed = (residue_mask[None, :] == 1) | (positions[:, None] == positions[None, :])
    allowed = allowed[None]
    highest = lax.optimization_barrier(jnp.max(jnp.where(allowed, scores, -jnp.inf), axis=-1, keepdims=True))
    raised = jnp.where(allowed, jnp.exp(scores - highest), 0.0)
    weights = (raised / lax.optimization_barrier(jnp.sum(raised, axis=-1, keepdims=True))).astype(jnp.bfloat16)
    gathered = jnp.einsum('hij,jhd->ihd', weights.astype(jnp.float32), values.astype(jnp.float32)).reshape(L, D)
    mixed = (gate * gathered).astype(jnp.bfloat16)
    update = jnp.dot(mixed, attention_out, preferred_element_type=jnp.float32)
    sequence_out = (sequence.astype(jnp.float32) + update).astype(jnp.bfloat16)
    normed_out = layer_norm(sequence_out.astype(jnp.float32)).astype(jnp.bfloat16)
    outer_rows = jnp.dot(normed_out, outer_in, preferred_element_type=jnp.float32).astype(jnp.bfloat16)
    left_side = outer_rows[:, :P_SIZE].astype(jnp.float32)
    right_side = outer_rows[:, P_SIZE:].astype(jnp.float32)
    outer_feat = jnp.concatenate([left_side[:, None, :] * right_side[None, :, :], left_side[:, None, :] - right_side[None, :, :]], axis=-1).astype(jnp.bfloat16)
    pair_mid = pair_wide + jnp.einsum('ijc,ce->ije', outer_feat.astype(jnp.float32), outer_out.astype(jnp.float32))
    normed_mid = layer_norm(pair_mid).astype(jnp.bfloat16)
    live = residue_mask.astype(jnp.float32)
    flat_in = triangle_in.reshape(C, 5 * C)

    def triangle_row(packed):
        row_normed, row_live = packed
        tri = jnp.dot(row_normed, flat_in, preferred_element_type=jnp.float32).reshape(L, 5, C)
        pair_live = (row_live * live)[:, None]
        left_row = (jax.nn.sigmoid(tri[:, 0]) * tri[:, 1] * pair_live).astype(jnp.bfloat16)
        right_row = (jax.nn.sigmoid(tri[:, 2]) * tri[:, 3] * pair_live).astype(jnp.bfloat16)
        return (left_row, right_row, jax.nn.sigmoid(tri[:, 4]))
    left_op, right_op, out_gate = lax.map(triangle_row, (normed_mid, live))
    product = jnp.einsum('ikc,jkc->ijc', left_op.astype(jnp.float32), right_op.astype(jnp.float32))
    normed_product = layer_norm(product).astype(jnp.bfloat16)
    pair_late = pair_mid + out_gate * jnp.einsum('ijc,ce->ije', normed_product.astype(jnp.float32), triangle_out.astype(jnp.float32))
    normed_late = layer_norm(pair_late).astype(jnp.bfloat16)

    def transition_row(row_normed):
        hidden = jax.nn.relu(jnp.dot(row_normed, transition_up, preferred_element_type=jnp.float32)).astype(jnp.bfloat16)
        return jnp.dot(hidden, transition_down, preferred_element_type=jnp.float32)
    pair_out = (pair_late + lax.map(transition_row, normed_late)).astype(jnp.bfloat16)
    return (sequence_out, pair_out)
```

```python
import functools
import math

import jax
import jax.numpy as jnp
from jax import lax
from jax.experimental import pallas as pl
from jax.experimental.pallas import tpu as pltpu
from jax.sharding import PartitionSpec as P

F32 = jnp.float32
BF16 = jnp.bfloat16
MESH = pl.DeviceIdType.MESH


def layer_norm(values):
    center = values - jnp.mean(values, axis=-1, keepdims=True)
    spread = jnp.mean(center * center, axis=-1, keepdims=True)
    return center * lax.rsqrt(spread + 1e-05)


def nt_dot(a, b):
    return lax.dot_general(a, b, (((1,), (1,)), ((), ())), preferred_element_type=F32)


def kernel(
    nr,
    nc,
    head_width,
    seq_ref,
    pair_ref,
    mask_ref,
    chain_ref,
    proj_ref,
    attn_out_ref,
    bias_w_ref,
    chain_bias_ref,
    outer_in_ref,
    outer_out_ref,
    tri_in_ref,
    tri_out_ref,
    up_ref,
    down_ref,
    seq_out_ref,
    pair_out_ref,
    bias_send,
    bias_recv,
    kv_all,
    base_scores,
    upd,
    outer_all,
    mid_ref,
    norm_ref,
    left_ref,
    right_ref,
    gate_ref,
    right_all,
    prod_ref,
    prod_recv,
    row_send,
    row_recv,
    col_send,
    col_recv,
):
    me_r = lax.axis_index("row")
    me_c = lax.axis_index("col")
    rows, width = seq_ref.shape
    pairs, chan = pair_ref.shape
    cols = pairs // rows
    length = mask_ref.shape[1]
    feats = attn_out_ref.shape[0]
    heads = feats // head_width
    heads_all = chain_bias_ref.shape[1]
    per_col = cols // rows
    row_start = me_r * rows
    col_start = me_c * cols

    def row_peer(d):
        return lax.rem(me_r + d, nr)

    def col_peer(d):
        return lax.rem(me_c + d, nc)

    def row_copy(phase, d, src, dst):
        return pltpu.make_async_remote_copy(
            src_ref=src,
            dst_ref=dst,
            send_sem=row_send.at[phase, d],
            recv_sem=row_recv.at[phase, d],
            device_id=(row_peer(d), me_c),
            device_id_type=MESH,
        )

    def col_copy(phase, d, src, dst):
        return pltpu.make_async_remote_copy(
            src_ref=src,
            dst_ref=dst,
            send_sem=col_send.at[phase, d],
            recv_sem=col_recv.at[phase, d],
            device_id=(me_r, col_peer(d)),
            device_id_type=MESH,
        )

    barrier = pltpu.get_barrier_semaphore()
    for d in range(1, nr):
        pl.semaphore_signal(barrier, inc=1, device_id=(row_peer(d), me_c), device_id_type=MESH)
    for d in range(1, nc):
        pl.semaphore_signal(barrier, inc=1, device_id=(me_r, col_peer(d)), device_id_type=MESH)

    my_rows = pl.ds(pl.multiple_of(row_start, rows), rows)
    kv_all[my_rows, :] = proj_ref[:, feats : 3 * feats].astype(BF16)
    pl.semaphore_wait(barrier, nr + nc - 2)
    kv_copies = []
    for d in range(1, nr):
        kv_copies.append(row_copy(0, d, kv_all.at[my_rows, :], kv_all.at[my_rows, :]))
        kv_copies[-1].start()
    normed_pair = layer_norm(pair_ref[...].astype(F32)).astype(BF16)
    bias_t = bias_w_ref[...].astype(F32).T.astype(BF16)
    tile = nt_dot(bias_t, normed_pair)
    for c in range(nc):
        bias_send[c] = tile[c * heads : (c + 1) * heads, :]
    bias_copies = []
    for d in range(1, nc):
        bias_copies.append(col_copy(0, d, bias_send.at[col_peer(d)], bias_recv.at[me_c]))
        bias_copies[-1].start()
    bias_recv[me_c] = bias_send[me_c]

    lane_l = lax.broadcasted_iota(jnp.int32, (rows, length), 1)
    sub_l = lax.broadcasted_iota(jnp.int32, (rows, length), 0)
    mine = lane_l == sub_l + row_start
    chain_row = chain_ref[...]
    mask_row = mask_ref[...]
    chain_col = jnp.sum(
        jnp.where(mine, chain_row.astype(F32), 0.0), axis=-1, keepdims=True
    )
    allowed = jnp.logical_or(mask_row == 1, mine)
    same = (chain_col == chain_row.astype(F32)).astype(F32)
    blocked = jnp.where(allowed, 0.0, -jnp.inf)
    hl = lax.broadcasted_iota(jnp.int32, (heads, heads_all), 1)
    hs = lax.broadcasted_iota(jnp.int32, (heads, heads_all), 0)
    offset = jnp.sum(
        jnp.where(hl == hs + me_c * heads, chain_bias_ref[...], 0.0), axis=-1, keepdims=True
    )
    head_lane = lax.broadcasted_iota(jnp.int32, (heads, feats), 1) // head_width
    own_head = head_lane == lax.broadcasted_iota(jnp.int32, (heads, feats), 0)
    query = proj_ref[:, :feats].astype(BF16).astype(F32)
    gate = jax.nn.sigmoid(proj_ref[:, 3 * feats :])
    query_big = jnp.concatenate(
        [jnp.where(own_head, query[i : i + 1, :], 0.0) for i in range(rows)], axis=0
    ).astype(BF16)

    for copy in bias_copies:
        copy.wait()
    lanes = 128
    per_vreg = lanes // cols
    lane_v = lax.broadcasted_iota(jnp.int32, (heads, lanes), 1) // cols
    for i in range(rows):
        g, s = divmod(i, per_vreg)
        for t in range(length // lanes):
            got = None
            for q in range(per_vreg):
                piece = bias_recv[t * per_vreg + q, :, g * lanes : (g + 1) * lanes]
                shift = (q - s) % per_vreg * cols
                if shift:
                    piece = pltpu.roll(piece, shift, 1)
                got = piece if got is None else jnp.where(lane_v == q, piece, got)
            window = slice(t * lanes, (t + 1) * lanes)
            base_scores[i * heads : (i + 1) * heads, window] = (
                got + offset * same[i : i + 1, window] + blocked[i : i + 1, window]
            )
    for copy in kv_copies:
        copy.wait()
    scores = nt_dot(query_big, kv_all[:, :feats]) * (1.0 / math.sqrt(head_width))
    scores = scores + base_scores[...]
    highest = jnp.max(scores, axis=-1, keepdims=True)
    raised = jnp.exp(scores - highest)
    weights = (raised / jnp.sum(raised, axis=-1, keepdims=True)).astype(BF16)
    spread_out = jnp.dot(weights, kv_all[:, feats:], preferred_element_type=F32)
    gathered = jnp.concatenate(
        [
            jnp.sum(
                jnp.where(own_head, spread_out[i * heads : (i + 1) * heads, :], 0.0),
                axis=0,
                keepdims=True,
            )
            for i in range(rows)
        ],
        axis=0,
    )
    mixed = (gate * gathered).astype(BF16)
    upd[me_c] = jnp.dot(mixed, attn_out_ref[...], preferred_element_type=F32).astype(BF16)
    upd_copies = []
    for d in range(1, nc):
        upd_copies.append(col_copy(1, d, upd.at[me_c], upd.at[me_c]))
        upd_copies[-1].start()
    for copy in upd_copies:
        copy.wait()
    update = upd[0].astype(F32)
    for c in range(1, nc):
        update = update + upd[c].astype(F32)
    sequence_out = (seq_ref[...].astype(F32) + update).astype(BF16)
    seq_out_ref[...] = sequence_out
    normed_out = layer_norm(sequence_out.astype(F32)).astype(BF16)
    outer_rows = jnp.dot(normed_out, outer_in_ref[...], preferred_element_type=F32).astype(BF16)
    outer_all[my_rows, :] = outer_rows
    outer_copies = []
    for d in range(1, nr):
        outer_copies.append(row_copy(1, d, outer_all.at[my_rows, :], outer_all.at[my_rows, :]))
        outer_copies[-1].start()
    half = outer_rows.shape[1] // 2
    left_rows = outer_rows.astype(F32)
    low_r = lax.broadcasted_iota(jnp.int32, (rows, 2 * half), 1) < half
    left_rows = jnp.where(low_r, left_rows, pltpu.roll(left_rows, half, 1))
    live_row = mask_row.astype(F32)
    live_i = jnp.sum(jnp.where(mine, live_row, 0.0), axis=-1, keepdims=True)
    lane_c = lax.broadcasted_iota(jnp.int32, (cols, length), 1)
    sub_c = lax.broadcasted_iota(jnp.int32, (cols, length), 0)
    live_k = jnp.sum(
        jnp.where(lane_c == sub_c + col_start, live_row, 0.0), axis=-1, keepdims=True
    )
    for copy in outer_copies:
        copy.wait()
    right_rows = outer_all[pl.ds(pl.multiple_of(col_start, cols), cols), :].astype(F32)
    low_c = lax.broadcasted_iota(jnp.int32, (cols, 2 * half), 1) < half
    right_rows = jnp.where(low_c, pltpu.roll(right_rows, half, 1), right_rows)
    for i in range(rows):
        left_i = left_rows[i : i + 1, :]
        feat = jnp.where(low_c, left_i * right_rows, left_i - right_rows).astype(BF16)
        norm_ref[i * cols : (i + 1) * cols, :] = feat
    mid = pair_ref[...].astype(F32) + jnp.dot(
        norm_ref[...], outer_out_ref[...], preferred_element_type=F32
    )
    mid_ref[...] = mid
    normed_mid = layer_norm(mid).astype(BF16)
    norm_ref[...] = normed_mid

    tri_r = jnp.dot(
        normed_mid, tri_in_ref[:, 2 * chan : 4 * chan], preferred_element_type=F32
    )
    right_ref[...] = jax.nn.sigmoid(tri_r[:, :chan]) * tri_r[:, chan:]
    for k in range(cols):
        block = right_ref[pl.ds(k, rows, stride=cols), :]
        right_all[me_r, k] = (block * (live_i * live_k[k : k + 1, :])).astype(BF16)
    right_copies = []
    for d in range(1, nr):
        right_copies.append(row_copy(2, d, right_all.at[me_r], right_all.at[me_r]))
        right_copies[-1].start()
    tri_l = jnp.dot(norm_ref[...], tri_in_ref[:, : 2 * chan], preferred_element_type=F32)
    left_raw = jax.nn.sigmoid(tri_l[:, :chan]) * tri_l[:, chan:]
    for i in range(rows):
        window = slice(i * cols, (i + 1) * cols)
        left_ref[window, :] = (
            (left_raw[window, :] * (live_i[i : i + 1, :] * live_k)).astype(BF16).astype(F32)
        )
    gate_ref[...] = jax.nn.sigmoid(
        jnp.dot(norm_ref[...], tri_in_ref[:, 4 * chan :], preferred_element_type=F32)
    )

    def one_block(slot):
        def step(k, sums):
            right_k = right_all[slot, k].astype(F32)
            return tuple(
                sums[i] + left_ref[pl.ds(i * cols + k, 1), :] * right_k for i in range(rows)
            )

        sums = lax.fori_loop(
            0, cols, step, tuple(jnp.zeros((rows, chan), F32) for _ in range(rows))
        )
        for i in range(rows):
            prod_ref[slot, i] = sums[i].astype(BF16)

    one_block(me_r)
    for d in range(1, nr):
        right_copies[d - 1].wait()
        one_block(lax.rem(me_r + nr - d, nr))
    prod_copies = []
    for d in range(1, nc):
        theirs = pl.ds(col_peer(d) * per_col, per_col)
        prod_copies.append(col_copy(2, d, prod_ref.at[theirs], prod_recv.at[me_c]))
        prod_copies[-1].start()
    prod_recv[me_c] = prod_ref[pl.ds(me_c * per_col, per_col)]
    for copy in prod_copies:
        copy.wait()
    for i in range(rows):
        for b in range(per_col):
            total = prod_recv[0, b, i].astype(F32)
            for c in range(1, nc):
                total = total + prod_recv[c, b, i].astype(F32)
            start = i * cols + b * rows
            norm_ref[start : start + rows, :] = layer_norm(total).astype(BF16)
    late = mid_ref[...] + gate_ref[...] * jnp.dot(
        norm_ref[...], tri_out_ref[...], preferred_element_type=F32
    )
    normed_late = layer_norm(late).astype(BF16)
    hidden = jnp.maximum(
        jnp.dot(normed_late, up_ref[...], preferred_element_type=F32), 0.0
    ).astype(BF16)
    lowered = jnp.dot(hidden, down_ref[...], preferred_element_type=F32)
    pair_out_ref[...] = (late + lowered).astype(BF16)


def per_device(
    nr,
    nc,
    sequence,
    pair_state,
    residue_mask,
    chain_index,
    attention_in,
    attention_out,
    bias_weight,
    chain_bias,
    outer_in,
    outer_out,
    triangle_in,
    triangle_out,
    transition_up,
    transition_down,
):
    rows, cols, chan = pair_state.shape
    width = sequence.shape[1]
    length = residue_mask.shape[0]
    feats = attention_out.shape[0]
    heads_all = chain_bias.shape[0]
    heads = heads_all // nc
    head_width = feats // heads
    normed_seq = layer_norm(sequence.astype(F32)).astype(BF16)
    projected = jnp.einsum(
        "id,dpe->ipe", normed_seq, attention_in, preferred_element_type=F32
    ).reshape(rows, 4 * feats)
    pairs = rows * cols
    per_col = cols // rows
    vmem = pl.BlockSpec(memory_space=pltpu.VMEM)
    sequence_out, pair_out = pl.pallas_call(
        functools.partial(kernel, nr, nc, head_width),
        out_shape=(
            jax.ShapeDtypeStruct((rows, width), BF16),
            jax.ShapeDtypeStruct((pairs, chan), BF16),
        ),
        in_specs=[vmem] * 14,
        out_specs=(vmem, vmem),
        scratch_shapes=[
            pltpu.VMEM((nc, heads, pairs), F32),
            pltpu.VMEM((nc, heads, pairs), F32),
            pltpu.VMEM((length, 2 * feats), BF16),
            pltpu.VMEM((rows * heads, length), F32),
            pltpu.VMEM((nc, rows, width), BF16),
            pltpu.VMEM((length, outer_in.shape[1]), BF16),
            pltpu.VMEM((pairs, chan), F32),
            pltpu.VMEM((pairs, chan), BF16),
            pltpu.VMEM((pairs, chan), F32),
            pltpu.VMEM((pairs, chan), F32),
            pltpu.VMEM((pairs, chan), F32),
            pltpu.VMEM((nr, cols, rows, chan), BF16),
            pltpu.VMEM((nr, rows, rows, chan), BF16),
            pltpu.VMEM((nc, per_col, rows, rows, chan), BF16),
            pltpu.SemaphoreType.DMA((3, nr)),
            pltpu.SemaphoreType.DMA((3, nr)),
            pltpu.SemaphoreType.DMA((3, nc)),
            pltpu.SemaphoreType.DMA((3, nc)),
        ],
        compiler_params=pltpu.CompilerParams(
            collective_id=0, has_side_effects=True, vmem_limit_bytes=48 * 1024 * 1024
        ),
    )(
        sequence,
        pair_state.reshape(pairs, chan),
        residue_mask.reshape(1, length),
        chain_index.reshape(1, length),
        projected,
        attention_out,
        bias_weight,
        chain_bias.reshape(1, heads_all),
        outer_in,
        outer_out,
        triangle_in.reshape(chan, 5 * chan),
        triangle_out,
        transition_up,
        transition_down,
    )
    return sequence_out, pair_out.reshape(rows, cols, chan)


def solution(mesh):
    return jax.shard_map(
        functools.partial(per_device, mesh.shape["row"], mesh.shape["col"]),
        mesh=mesh,
        in_specs=(
            P("row", None),
            P("row", "col", None),
            P(),
            P(),
            P(None, None, "col"),
            P("col", None),
            P(),
            P(),
            P(),
            P(),
            P(),
            P(),
            P(),
            P(),
        ),
        out_specs=(P("row", None), P("row", "col", None)),
        check_vma=False,
    )
```

```python
import functools
import math

import jax
import jax.numpy as jnp
from jax import lax
from jax.experimental import pallas as pl
from jax.experimental.pallas import tpu as pltpu
from jax.sharding import PartitionSpec as P

F32 = jnp.float32
BF16 = jnp.bfloat16
MESH = pl.DeviceIdType.MESH


def layer_norm(values):
    center = values - jnp.mean(values, axis=-1, keepdims=True)
    spread = jnp.mean(center * center, axis=-1, keepdims=True)
    return center * lax.rsqrt(spread + 1e-05)


def nt_dot(a, b):
    return lax.dot_general(a, b, (((1,), (1,)), ((), ())), preferred_element_type=F32)


def kernel(
    nr,
    nc,
    head_width,
    seq_ref,
    pair_ref,
    mask_ref,
    chain_ref,
    proj_ref,
    attn_out_ref,
    bias_w_ref,
    chain_bias_ref,
    outer_in_ref,
    tri_in_ref,
    outer_out_hbm,
    tri_out_hbm,
    up_hbm,
    down_hbm,
    seq_out_ref,
    pair_out_ref,
    bias_send,
    bias_recv,
    kv_all,
    base_scores,
    upd,
    outer_all,
    mid_ref,
    norm_ref,
    left_ref,
    left_send,
    left_recv,
    right_ref,
    gate_ref,
    right_all,
    prod_ref,
    prod_recv,
    outer_out_ref,
    tri_out_ref,
    up_ref,
    down_ref,
    row_send,
    row_recv,
    col_send,
    col_recv,
    prod_send_sem,
    prod_recv_sem,
    load_sem,
):
    me_r = lax.axis_index("row")
    me_c = lax.axis_index("col")
    rows, width = seq_ref.shape
    pairs, chan = pair_ref.shape
    cols = pairs // rows
    length = mask_ref.shape[1]
    feats = attn_out_ref.shape[0]
    heads = feats // head_width
    heads_all = chain_bias_ref.shape[1]
    per_col = cols // rows
    row_start = me_r * rows
    col_start = me_c * cols
    parity = lax.rem(me_r, 2)
    partner = me_r + 1 - 2 * parity
    line = nr // 2
    me_z = me_r // 2
    share = per_col // 2

    loads = [
        pltpu.make_async_copy(src, dst, load_sem.at[n])
        for n, (src, dst) in enumerate(
            (
                (outer_out_hbm, outer_out_ref),
                (tri_out_hbm, tri_out_ref),
                (up_hbm, up_ref),
                (down_hbm, down_ref),
            )
        )
    ]
    for load in loads:
        load.start()

    def row_peer(d):
        return lax.rem(me_r + d, nr)

    def col_peer(d):
        return lax.rem(me_c + d, nc)

    def row_copy(phase, d, src, dst):
        return pltpu.make_async_remote_copy(
            src_ref=src,
            dst_ref=dst,
            send_sem=row_send.at[phase, d],
            recv_sem=row_recv.at[phase, d],
            device_id=(row_peer(d), me_c),
            device_id_type=MESH,
        )

    def col_copy(phase, d, src, dst):
        return pltpu.make_async_remote_copy(
            src_ref=src,
            dst_ref=dst,
            send_sem=col_send.at[phase, d],
            recv_sem=col_recv.at[phase, d],
            device_id=(me_r, col_peer(d)),
            device_id_type=MESH,
        )

    barrier = pltpu.get_barrier_semaphore()
    for d in range(1, nr):
        pl.semaphore_signal(barrier, inc=1, device_id=(row_peer(d), me_c), device_id_type=MESH)
    for d in range(1, nc):
        pl.semaphore_signal(barrier, inc=1, device_id=(me_r, col_peer(d)), device_id_type=MESH)
        pl.semaphore_signal(barrier, inc=1, device_id=(partner, col_peer(d)), device_id_type=MESH)

    my_rows = pl.ds(pl.multiple_of(row_start, rows), rows)
    kv_all[my_rows, :] = proj_ref[:, feats : 3 * feats].astype(BF16)
    normed_pair = layer_norm(pair_ref[...].astype(F32)).astype(BF16)
    tile = nt_dot(bias_w_ref[...], normed_pair)
    for c in range(nc):
        bias_send[c] = tile[c * heads : (c + 1) * heads, :]
    pl.semaphore_wait(barrier, nr + 2 * nc - 3)
    kv_copies = []
    for d in range(1, nr):
        kv_copies.append(row_copy(0, d, kv_all.at[my_rows, :], kv_all.at[my_rows, :]))
        kv_copies[-1].start()
    bias_copies = []
    for d in range(1, nc):
        bias_copies.append(col_copy(0, d, bias_send.at[col_peer(d)], bias_recv.at[me_c]))
        bias_copies[-1].start()
    bias_recv[me_c] = bias_send[me_c]

    lane_l = lax.broadcasted_iota(jnp.int32, (rows, length), 1)
    sub_l = lax.broadcasted_iota(jnp.int32, (rows, length), 0)
    mine = lane_l == sub_l + row_start
    chain_row = chain_ref[...]
    mask_row = mask_ref[...]
    chain_col = jnp.sum(
        jnp.where(mine, chain_row.astype(F32), 0.0), axis=-1, keepdims=True
    )
    allowed = jnp.logical_or(mask_row == 1, mine)
    same = (chain_col == chain_row.astype(F32)).astype(F32)
    blocked = jnp.where(allowed, 0.0, -jnp.inf)
    hl = lax.broadcasted_iota(jnp.int32, (heads, heads_all), 1)
    hs = lax.broadcasted_iota(jnp.int32, (heads, heads_all), 0)
    offset = jnp.sum(
        jnp.where(hl == hs + me_c * heads, chain_bias_ref[...], 0.0), axis=-1, keepdims=True
    )
    head_lane = lax.broadcasted_iota(jnp.int32, (heads, feats), 1) // head_width
    own_head = head_lane == lax.broadcasted_iota(jnp.int32, (heads, feats), 0)
    query = proj_ref[:, :feats].astype(BF16).astype(F32)
    gate = jax.nn.sigmoid(proj_ref[:, 3 * feats :])
    query_big = jnp.concatenate(
        [jnp.where(own_head, query[i : i + 1, :], 0.0) for i in range(rows)], axis=0
    ).astype(BF16)

    for copy in bias_copies:
        copy.wait()
    lanes = 128
    per_vreg = lanes // cols
    lane_v = lax.broadcasted_iota(jnp.int32, (heads, lanes), 1) // cols
    for i in range(rows):
        g, s = divmod(i, per_vreg)
        for t in range(length // lanes):
            got = None
            for q in range(per_vreg):
                piece = bias_recv[t * per_vreg + q, :, g * lanes : (g + 1) * lanes]
                shift = (q - s) % per_vreg * cols
                if shift:
                    piece = pltpu.roll(piece, shift, 1)
                got = piece if got is None else jnp.where(lane_v == q, piece, got)
            window = slice(t * lanes, (t + 1) * lanes)
            base_scores[i * heads : (i + 1) * heads, window] = (
                got + offset * same[i : i + 1, window] + blocked[i : i + 1, window]
            )
    for copy in kv_copies:
        copy.wait()
    scores = nt_dot(query_big, kv_all[:, :feats]) * (1.0 / math.sqrt(head_width))
    scores = scores + base_scores[...]
    highest = jnp.max(scores, axis=-1, keepdims=True)
    raised = jnp.exp(scores - highest)
    weights = (raised / jnp.sum(raised, axis=-1, keepdims=True)).astype(BF16)
    spread_out = jnp.dot(weights, kv_all[:, feats:], preferred_element_type=F32)
    gathered = jnp.concatenate(
        [
            jnp.sum(
                jnp.where(own_head, spread_out[i * heads : (i + 1) * heads, :], 0.0),
                axis=0,
                keepdims=True,
            )
            for i in range(rows)
        ],
        axis=0,
    )
    mixed = (gate * gathered).astype(BF16)
    upd[me_c] = jnp.dot(mixed, attn_out_ref[...], preferred_element_type=F32).astype(BF16)
    upd_copies = []
    for d in range(1, nc):
        upd_copies.append(col_copy(1, d, upd.at[me_c], upd.at[me_c]))
        upd_copies[-1].start()
    for copy in upd_copies:
        copy.wait()
    update = upd[0].astype(F32)
    for c in range(1, nc):
        update = update + upd[c].astype(F32)
    sequence_out = (seq_ref[...].astype(F32) + update).astype(BF16)
    seq_out_ref[...] = sequence_out
    normed_out = layer_norm(sequence_out.astype(F32)).astype(BF16)
    outer_rows = jnp.dot(normed_out, outer_in_ref[...], preferred_element_type=F32).astype(BF16)
    outer_all[my_rows, :] = outer_rows
    outer_copies = []
    for d in range(1, nr):
        outer_copies.append(row_copy(1, d, outer_all.at[my_rows, :], outer_all.at[my_rows, :]))
        outer_copies[-1].start()
    half = outer_rows.shape[1] // 2
    left_rows = outer_rows.astype(F32)
    low_r = lax.broadcasted_iota(jnp.int32, (rows, 2 * half), 1) < half
    left_rows = jnp.where(low_r, left_rows, pltpu.roll(left_rows, half, 1))
    live_row = mask_row.astype(F32)
    live_i = jnp.sum(jnp.where(mine, live_row, 0.0), axis=-1, keepdims=True)
    lane_c = lax.broadcasted_iota(jnp.int32, (cols, length), 1)
    sub_c = lax.broadcasted_iota(jnp.int32, (cols, length), 0)
    live_k = jnp.sum(
        jnp.where(lane_c == sub_c + col_start, live_row, 0.0), axis=-1, keepdims=True
    )
    loads[0].wait()
    for copy in outer_copies:
        copy.wait()
    right_rows = outer_all[pl.ds(pl.multiple_of(col_start, cols), cols), :].astype(F32)
    low_c = lax.broadcasted_iota(jnp.int32, (cols, 2 * half), 1) < half
    right_rows = jnp.where(low_c, pltpu.roll(right_rows, half, 1), right_rows)
    for i in range(rows):
        left_i = left_rows[i : i + 1, :]
        feat = jnp.where(low_c, left_i * right_rows, left_i - right_rows).astype(BF16)
        norm_ref[i * cols : (i + 1) * cols, :] = feat
    mid = pair_ref[...].astype(F32) + jnp.dot(
        norm_ref[...], outer_out_ref[...], preferred_element_type=F32
    )
    mid_ref[...] = mid
    normed_mid = layer_norm(mid).astype(BF16)
    norm_ref[...] = normed_mid

    tri_g = jnp.dot(normed_mid, tri_in_ref[2], preferred_element_type=F32)
    tri_v = jnp.dot(normed_mid, tri_in_ref[3], preferred_element_type=F32)
    right_ref[...] = jax.nn.sigmoid(tri_g) * tri_v
    for k in range(cols):
        block = right_ref[pl.ds(k, rows, stride=cols), :]
        right_all[me_z, k] = (block * (live_i * live_k[k : k + 1, :])).astype(BF16)
    right_copies = []
    for d in range(1, line):
        right_copies.append(
            pltpu.make_async_remote_copy(
                src_ref=right_all.at[me_z],
                dst_ref=right_all.at[me_z],
                send_sem=row_send.at[2, d],
                recv_sem=row_recv.at[2, d],
                device_id=(lax.rem(me_z + d, line) * 2 + parity, me_c),
                device_id_type=MESH,
            )
        )
        right_copies[-1].start()
    tri_g = jnp.dot(norm_ref[...], tri_in_ref[0], preferred_element_type=F32)
    tri_v = jnp.dot(norm_ref[...], tri_in_ref[1], preferred_element_type=F32)
    left_raw = jax.nn.sigmoid(tri_g) * tri_v
    for i in range(rows):
        window = slice(i * cols, (i + 1) * cols)
        rounded = (left_raw[window, :] * (live_i[i : i + 1, :] * live_k)).astype(BF16)
        left_send[window, :] = rounded
        left_ref[0, window, :] = rounded.astype(F32)
    left_copy = pltpu.make_async_remote_copy(
        src_ref=left_send,
        dst_ref=left_recv,
        send_sem=row_send.at[2, 0],
        recv_sem=row_recv.at[2, 0],
        device_id=(partner, me_c),
        device_id_type=MESH,
    )
    left_copy.start()
    gate_ref[...] = jax.nn.sigmoid(
        jnp.dot(norm_ref[...], tri_in_ref[4], preferred_element_type=F32)
    )

    def owner_of(slot):
        block_row = slot * 2 + parity
        return block_row // per_col, lax.rem(block_row, per_col)

    def prod_copy(which, d, slot):
        owner, piece = owner_of(slot)
        apart = lax.rem(me_c + nc - owner, nc)
        return pltpu.make_async_remote_copy(
            src_ref=prod_ref.at[which, slot],
            dst_ref=prod_recv.at[me_c, piece],
            send_sem=prod_send_sem.at[which, d],
            recv_sem=prod_recv_sem.at[which, apart * share + piece // 2],
            device_id=(partner if which else me_r, owner),
            device_id_type=MESH,
        )

    def one_block(which, d, slot):
        def step(k, sums):
            right_k = right_all[slot, k].astype(F32)
            return tuple(
                sums[i] + left_ref[which, pl.ds(i * cols + k, 1), :] * right_k
                for i in range(rows)
            )

        sums = lax.fori_loop(
            0, cols, step, tuple(jnp.zeros((rows, chan), F32) for _ in range(rows))
        )
        for i in range(rows):
            prod_ref[which, slot, i] = sums[i].astype(BF16)
        if which:
            prod_copy(which, d, slot).start()
        else:
            owner, piece = owner_of(slot)

            @pl.when(owner != me_c)
            def _():
                prod_copy(which, d, slot).start()

            @pl.when(owner == me_c)
            def _():
                prod_recv[me_c, piece] = prod_ref[which, slot]

    slots = [lax.rem(me_z + line - d, line) for d in range(line)]
    one_block(0, 0, slots[0])
    left_copy.wait()
    left_ref[1] = left_recv[...].astype(F32)
    one_block(1, 0, slots[0])
    for d in range(1, line):
        right_copies[d - 1].wait()
        one_block(1, d, slots[d])
        one_block(0, d, slots[d])
    for e in range(nc):
        source = lax.rem(me_c + e, nc)
        for q in range(share):
            for which in range(2):
                if e or which:
                    piece = 2 * q + (1 - parity if which else parity)
                    pltpu.make_async_remote_copy(
                        src_ref=prod_ref.at[which, 0],
                        dst_ref=prod_recv.at[source, piece],
                        send_sem=prod_send_sem.at[which, 0],
                        recv_sem=prod_recv_sem.at[which, e * share + q],
                        device_id=(partner, me_c),
                        device_id_type=MESH,
                    ).wait_recv()
    for d in range(line):
        prod_copy(1, d, slots[d]).wait_send()
        owner, _ = owner_of(slots[d])

        @pl.when(owner != me_c)
        def _():
            prod_copy(0, d, slots[d]).wait_send()

    for load in loads[1:]:
        load.wait()
    for i in range(rows):
        for b in range(per_col):
            total = prod_recv[0, b, i].astype(F32)
            for c in range(1, nc):
                total = total + prod_recv[c, b, i].astype(F32)
            start = i * cols + b * rows
            norm_ref[start : start + rows, :] = layer_norm(total).astype(BF16)
    late = mid_ref[...] + gate_ref[...] * jnp.dot(
        norm_ref[...], tri_out_ref[...], preferred_element_type=F32
    )
    normed_late = layer_norm(late).astype(BF16)
    hidden = jnp.maximum(
        jnp.dot(normed_late, up_ref[...], preferred_element_type=F32), 0.0
    ).astype(BF16)
    lowered = jnp.dot(hidden, down_ref[...], preferred_element_type=F32)
    pair_out_ref[...] = (late + lowered).astype(BF16)


def per_device(
    nr,
    nc,
    sequence,
    pair_state,
    residue_mask,
    chain_index,
    attention_in,
    attention_out,
    bias_weight,
    chain_bias,
    outer_in,
    outer_out,
    triangle_in,
    triangle_out,
    transition_up,
    transition_down,
):
    rows, cols, chan = pair_state.shape
    width = sequence.shape[1]
    length = residue_mask.shape[0]
    feats = attention_out.shape[0]
    heads_all = chain_bias.shape[0]
    heads = heads_all // nc
    head_width = feats // heads
    normed_seq = layer_norm(sequence.astype(F32)).astype(BF16)
    projected = jnp.einsum(
        "id,dpe->ipe", normed_seq, attention_in, preferred_element_type=F32
    ).reshape(rows, 4 * feats)
    pairs = rows * cols
    per_col = cols // rows
    vmem = pl.BlockSpec(memory_space=pltpu.VMEM)
    sequence_out, pair_out = pl.pallas_call(
        functools.partial(kernel, nr, nc, head_width),
        out_shape=(
            jax.ShapeDtypeStruct((rows, width), BF16),
            jax.ShapeDtypeStruct((pairs, chan), BF16),
        ),
        in_specs=[vmem] * 10 + [pl.BlockSpec(memory_space=pltpu.HBM)] * 4,
        out_specs=(vmem, vmem),
        scratch_shapes=[
            pltpu.VMEM((nc, heads, pairs), F32),
            pltpu.VMEM((nc, heads, pairs), F32),
            pltpu.VMEM((length, 2 * feats), BF16),
            pltpu.VMEM((rows * heads, length), F32),
            pltpu.VMEM((nc, rows, width), BF16),
            pltpu.VMEM((length, outer_in.shape[1]), BF16),
            pltpu.VMEM((pairs, chan), F32),
            pltpu.VMEM((pairs, chan), BF16),
            pltpu.VMEM((2, pairs, chan), F32),
            pltpu.VMEM((pairs, chan), BF16),
            pltpu.VMEM((pairs, chan), BF16),
            pltpu.VMEM((pairs, chan), F32),
            pltpu.VMEM((pairs, chan), F32),
            pltpu.VMEM((nr // 2, cols, rows, chan), BF16),
            pltpu.VMEM((2, nr // 2, rows, rows, chan), BF16),
            pltpu.VMEM((nc, per_col, rows, rows, chan), BF16),
            pltpu.VMEM(outer_out.shape, BF16),
            pltpu.VMEM(triangle_out.shape, BF16),
            pltpu.VMEM(transition_up.shape, BF16),
            pltpu.VMEM(transition_down.shape, BF16),
            pltpu.SemaphoreType.DMA((3, nr)),
            pltpu.SemaphoreType.DMA((3, nr)),
            pltpu.SemaphoreType.DMA((2, nc)),
            pltpu.SemaphoreType.DMA((2, nc)),
            pltpu.SemaphoreType.DMA((2, nr // 2)),
            pltpu.SemaphoreType.DMA((2, nc * (per_col // 2))),
            pltpu.SemaphoreType.DMA((4,)),
        ],
        compiler_params=pltpu.CompilerParams(
            collective_id=0, has_side_effects=True, vmem_limit_bytes=48 * 1024 * 1024
        ),
    )(
        sequence,
        pair_state.reshape(pairs, chan),
        residue_mask.reshape(1, length),
        chain_index.reshape(1, length),
        projected,
        attention_out,
        bias_weight.T,
        chain_bias.reshape(1, heads_all),
        outer_in,
        jnp.transpose(triangle_in, (1, 0, 2)),
        outer_out,
        triangle_out,
        transition_up,
        transition_down,
    )
    return sequence_out, pair_out.reshape(rows, cols, chan)


def solution(mesh):
    return jax.shard_map(
        functools.partial(per_device, mesh.shape["row"], mesh.shape["col"]),
        mesh=mesh,
        in_specs=(
            P("row", None),
            P("row", "col", None),
            P(),
            P(),
            P(None, None, "col"),
            P("col", None),
            P(),
            P(),
            P(),
            P(),
            P(),
            P(),
            P(),
            P(),
        ),
        out_specs=(P("row", None), P("row", "col", None)),
        check_vma=False,
    )
```

```python
import functools
import math

import jax
import jax.numpy as jnp
from jax import lax
from jax.experimental import pallas as pl
from jax.experimental.pallas import tpu as pltpu
from jax.sharding import PartitionSpec as P

F32 = jnp.float32
BF16 = jnp.bfloat16
MESH = pl.DeviceIdType.MESH


def layer_norm(values):
    center = values - jnp.mean(values, axis=-1, keepdims=True)
    spread = jnp.mean(center * center, axis=-1, keepdims=True)
    return center * lax.rsqrt(spread + 1e-05)


def nt_dot(a, b):
    return lax.dot_general(a, b, (((1,), (1,)), ((), ())), preferred_element_type=F32)


def kernel(
    nr,
    nc,
    head_width,
    seq_hbm,
    pair_hbm,
    mask_hbm,
    chain_hbm,
    attn_in_hbm,
    attn_out_hbm,
    bias_w_hbm,
    chain_bias_hbm,
    outer_in_hbm,
    tri_in_hbm,
    outer_out_hbm,
    tri_out_hbm,
    up_hbm,
    down_hbm,
    seq_out_ref,
    pair_out_ref,
    bias_send,
    bias_recv,
    kv_all,
    base_scores,
    upd,
    outer_all,
    mid_ref,
    norm_ref,
    left_ref,
    left_send,
    left_recv,
    right_ref,
    gate_ref,
    right_all,
    prod_ref,
    prod_recv,
    seq_ref,
    pair_ref,
    mask_ref,
    chain_ref,
    attn_in_ref,
    attn_out_ref,
    bias_w_ref,
    chain_bias_ref,
    outer_in_ref,
    tri_in_ref,
    outer_out_ref,
    tri_out_ref,
    up_ref,
    down_ref,
    proj_ref,
    row_send,
    row_recv,
    col_send,
    col_recv,
    prod_send_sem,
    prod_recv_sem,
    load_sem,
):
    me_r = lax.axis_index("row")
    me_c = lax.axis_index("col")
    rows, width = seq_hbm.shape
    pairs, chan = pair_ref.shape
    cols = pairs // rows
    length = mask_ref.shape[1]
    feats = attn_out_ref.shape[0]
    heads = feats // head_width
    heads_all = chain_bias_ref.shape[1]
    per_col = cols // rows
    row_start = me_r * rows
    col_start = me_c * cols
    parity = lax.rem(me_r, 2)
    partner = me_r + 1 - 2 * parity
    line = nr // 2
    me_z = me_r // 2
    share = per_col // 2

    def row_peer(d):
        return lax.rem(me_r + d, nr)

    def col_peer(d):
        return lax.rem(me_c + d, nc)

    def row_copy(phase, d, src, dst):
        return pltpu.make_async_remote_copy(
            src_ref=src,
            dst_ref=dst,
            send_sem=row_send.at[phase, d],
            recv_sem=row_recv.at[phase, d],
            device_id=(row_peer(d), me_c),
            device_id_type=MESH,
        )

    def col_copy(phase, d, src, dst):
        return pltpu.make_async_remote_copy(
            src_ref=src,
            dst_ref=dst,
            send_sem=col_send.at[phase, d],
            recv_sem=col_recv.at[phase, d],
            device_id=(me_r, col_peer(d)),
            device_id_type=MESH,
        )

    barrier = pltpu.get_barrier_semaphore()
    for d in range(1, nr):
        pl.semaphore_signal(barrier, inc=1, device_id=(row_peer(d), me_c), device_id_type=MESH)
    for d in range(1, nc):
        pl.semaphore_signal(barrier, inc=1, device_id=(me_r, col_peer(d)), device_id_type=MESH)
        pl.semaphore_signal(barrier, inc=1, device_id=(partner, col_peer(d)), device_id_type=MESH)

    loads = {}
    for name, src, dst in (
        ("seq", seq_hbm, seq_ref),
        ("attn_in", attn_in_hbm, attn_in_ref),
        ("pair", pair_hbm, pair_ref),
        ("bias_w", bias_w_hbm, bias_w_ref),
        ("mask", mask_hbm, mask_ref),
        ("chain", chain_hbm, chain_ref),
        ("chain_bias", chain_bias_hbm, chain_bias_ref),
        ("attn_out", attn_out_hbm, attn_out_ref),
        ("outer_in", outer_in_hbm, outer_in_ref),
        ("outer_out", outer_out_hbm, outer_out_ref),
        ("tri_in", tri_in_hbm, tri_in_ref),
        ("tri_out", tri_out_hbm, tri_out_ref),
        ("up", up_hbm, up_ref),
        ("down", down_hbm, down_ref),
    ):
        loads[name] = pltpu.make_async_copy(src, dst, load_sem.at[len(loads)])
        loads[name].start()

    parts = attn_in_ref.shape[1]
    loads["seq"].wait()
    normed_seq = layer_norm(seq_ref[...].astype(F32)).astype(BF16)
    lane_w = 128
    pieces = width // lane_w
    stacked = jnp.concatenate(
        [normed_seq[:, n * lane_w : (n + 1) * lane_w] for n in range(pieces)], axis=0
    )
    spread_lane = lax.broadcasted_iota(jnp.int32, (lane_w, parts * lane_w), 1)
    spread_sub = lax.broadcasted_iota(jnp.int32, (lane_w, parts * lane_w), 0)
    spread = (spread_lane // parts == spread_sub).astype(F32).astype(BF16)
    repeated = jnp.dot(stacked, spread, preferred_element_type=F32)
    part_of = lax.broadcasted_iota(jnp.int32, (rows, parts * lane_w), 1) % parts
    loads["attn_in"].wait()
    projected = None
    for n in range(pieces):
        row_block = repeated[n * rows : (n + 1) * rows, :]
        masked = jnp.concatenate(
            [jnp.where(part_of == p, row_block, 0.0) for p in range(parts)], axis=0
        ).astype(BF16)
        weight = attn_in_ref[n * lane_w : (n + 1) * lane_w].reshape(parts * lane_w, feats)
        term = jnp.dot(masked, weight, preferred_element_type=F32)
        projected = term if projected is None else projected + term
    for p in range(parts):
        proj_ref[:, p * feats : (p + 1) * feats] = projected[p * rows : (p + 1) * rows, :]

    my_rows = pl.ds(pl.multiple_of(row_start, rows), rows)
    kv_all[my_rows, :] = proj_ref[:, feats : 3 * feats].astype(BF16)
    loads["pair"].wait()
    loads["bias_w"].wait()
    normed_pair = layer_norm(pair_ref[...].astype(F32)).astype(BF16)
    tile = nt_dot(bias_w_ref[...], normed_pair)
    for c in range(nc):
        bias_send[c] = tile[c * heads : (c + 1) * heads, :]
    pl.semaphore_wait(barrier, nr + 2 * nc - 3)
    kv_copies = []
    for d in range(1, nr):
        kv_copies.append(row_copy(0, d, kv_all.at[my_rows, :], kv_all.at[my_rows, :]))
        kv_copies[-1].start()
    bias_copies = []
    for d in range(1, nc):
        bias_copies.append(col_copy(0, d, bias_send.at[col_peer(d)], bias_recv.at[me_c]))
        bias_copies[-1].start()
    bias_recv[me_c] = bias_send[me_c]

    lane_l = lax.broadcasted_iota(jnp.int32, (rows, length), 1)
    sub_l = lax.broadcasted_iota(jnp.int32, (rows, length), 0)
    mine = lane_l == sub_l + row_start
    for name in ("mask", "chain", "chain_bias"):
        loads[name].wait()
    chain_row = chain_ref[...]
    mask_row = mask_ref[...]
    chain_col = jnp.sum(
        jnp.where(mine, chain_row.astype(F32), 0.0), axis=-1, keepdims=True
    )
    allowed = jnp.logical_or(mask_row == 1, mine)
    same = (chain_col == chain_row.astype(F32)).astype(F32)
    blocked = jnp.where(allowed, 0.0, -jnp.inf)
    hl = lax.broadcasted_iota(jnp.int32, (heads, heads_all), 1)
    hs = lax.broadcasted_iota(jnp.int32, (heads, heads_all), 0)
    offset = jnp.sum(
        jnp.where(hl == hs + me_c * heads, chain_bias_ref[...], 0.0), axis=-1, keepdims=True
    )
    head_lane = lax.broadcasted_iota(jnp.int32, (heads, feats), 1) // head_width
    own_head = head_lane == lax.broadcasted_iota(jnp.int32, (heads, feats), 0)
    query = proj_ref[:, :feats].astype(BF16).astype(F32)
    gate = jax.nn.sigmoid(proj_ref[:, 3 * feats :])
    query_big = jnp.concatenate(
        [jnp.where(own_head, query[i : i + 1, :], 0.0) for i in range(rows)], axis=0
    ).astype(BF16)

    for copy in bias_copies:
        copy.wait()
    lanes = 128
    per_vreg = lanes // cols
    lane_v = lax.broadcasted_iota(jnp.int32, (heads, lanes), 1) // cols
    for i in range(rows):
        g, s = divmod(i, per_vreg)
        for t in range(length // lanes):
            got = None
            for q in range(per_vreg):
                piece = bias_recv[t * per_vreg + q, :, g * lanes : (g + 1) * lanes]
                shift = (q - s) % per_vreg * cols
                if shift:
                    piece = pltpu.roll(piece, shift, 1)
                got = piece if got is None else jnp.where(lane_v == q, piece, got)
            window = slice(t * lanes, (t + 1) * lanes)
            base_scores[i * heads : (i + 1) * heads, window] = (
                got + offset * same[i : i + 1, window] + blocked[i : i + 1, window]
            )
    for copy in kv_copies:
        copy.wait()
    scores = nt_dot(query_big, kv_all[:, :feats]) * (1.0 / math.sqrt(head_width))
    scores = scores + base_scores[...]
    highest = jnp.max(scores, axis=-1, keepdims=True)
    raised = jnp.exp(scores - highest)
    weights = (raised / jnp.sum(raised, axis=-1, keepdims=True)).astype(BF16)
    spread_out = jnp.dot(weights, kv_all[:, feats:], preferred_element_type=F32)
    gathered = jnp.concatenate(
        [
            jnp.sum(
                jnp.where(own_head, spread_out[i * heads : (i + 1) * heads, :], 0.0),
                axis=0,
                keepdims=True,
            )
            for i in range(rows)
        ],
        axis=0,
    )
    mixed = (gate * gathered).astype(BF16)
    loads["attn_out"].wait()
    upd[me_c] = jnp.dot(mixed, attn_out_ref[...], preferred_element_type=F32).astype(BF16)
    upd_copies = []
    for d in range(1, nc):
        upd_copies.append(col_copy(1, d, upd.at[me_c], upd.at[me_c]))
        upd_copies[-1].start()
    for copy in upd_copies:
        copy.wait()
    update = upd[0].astype(F32)
    for c in range(1, nc):
        update = update + upd[c].astype(F32)
    sequence_out = (seq_ref[...].astype(F32) + update).astype(BF16)
    seq_out_ref[...] = sequence_out
    normed_out = layer_norm(sequence_out.astype(F32)).astype(BF16)
    loads["outer_in"].wait()
    outer_rows = jnp.dot(normed_out, outer_in_ref[...], preferred_element_type=F32).astype(BF16)
    outer_all[my_rows, :] = outer_rows
    outer_copies = []
    for d in range(1, nr):
        outer_copies.append(row_copy(1, d, outer_all.at[my_rows, :], outer_all.at[my_rows, :]))
        outer_copies[-1].start()
    half = outer_rows.shape[1] // 2
    left_rows = outer_rows.astype(F32)
    low_r = lax.broadcasted_iota(jnp.int32, (rows, 2 * half), 1) < half
    left_rows = jnp.where(low_r, left_rows, pltpu.roll(left_rows, half, 1))
    live_row = mask_row.astype(F32)
    live_i = jnp.sum(jnp.where(mine, live_row, 0.0), axis=-1, keepdims=True)
    lane_c = lax.broadcasted_iota(jnp.int32, (cols, length), 1)
    sub_c = lax.broadcasted_iota(jnp.int32, (cols, length), 0)
    live_k = jnp.sum(
        jnp.where(lane_c == sub_c + col_start, live_row, 0.0), axis=-1, keepdims=True
    )
    loads["outer_out"].wait()
    loads["tri_in"].wait()
    for copy in outer_copies:
        copy.wait()
    right_rows = outer_all[pl.ds(pl.multiple_of(col_start, cols), cols), :].astype(F32)
    low_c = lax.broadcasted_iota(jnp.int32, (cols, 2 * half), 1) < half
    right_rows = jnp.where(low_c, pltpu.roll(right_rows, half, 1), right_rows)
    for i in range(rows):
        left_i = left_rows[i : i + 1, :]
        feat = jnp.where(low_c, left_i * right_rows, left_i - right_rows).astype(BF16)
        norm_ref[i * cols : (i + 1) * cols, :] = feat
    mid = pair_ref[...].astype(F32) + jnp.dot(
        norm_ref[...], outer_out_ref[...], preferred_element_type=F32
    )
    mid_ref[...] = mid
    normed_mid = layer_norm(mid).astype(BF16)
    norm_ref[...] = normed_mid

    tri_g = jnp.dot(normed_mid, tri_in_ref[2], preferred_element_type=F32)
    tri_v = jnp.dot(normed_mid, tri_in_ref[3], preferred_element_type=F32)
    right_ref[...] = jax.nn.sigmoid(tri_g) * tri_v
    for k in range(cols):
        block = right_ref[pl.ds(k, rows, stride=cols), :]
        right_all[me_z, k] = (block * (live_i * live_k[k : k + 1, :])).astype(BF16)
    right_copies = []
    for d in range(1, line):
        right_copies.append(
            pltpu.make_async_remote_copy(
                src_ref=right_all.at[me_z],
                dst_ref=right_all.at[me_z],
                send_sem=row_send.at[2, d],
                recv_sem=row_recv.at[2, d],
                device_id=(lax.rem(me_z + d, line) * 2 + parity, me_c),
                device_id_type=MESH,
            )
        )
        right_copies[-1].start()
    tri_g = jnp.dot(norm_ref[...], tri_in_ref[0], preferred_element_type=F32)
    tri_v = jnp.dot(norm_ref[...], tri_in_ref[1], preferred_element_type=F32)
    left_raw = jax.nn.sigmoid(tri_g) * tri_v
    for i in range(rows):
        window = slice(i * cols, (i + 1) * cols)
        rounded = (left_raw[window, :] * (live_i[i : i + 1, :] * live_k)).astype(BF16)
        left_send[window, :] = rounded
        left_ref[0, window, :] = rounded.astype(F32)
    left_copy = pltpu.make_async_remote_copy(
        src_ref=left_send,
        dst_ref=left_recv,
        send_sem=row_send.at[2, 0],
        recv_sem=row_recv.at[2, 0],
        device_id=(partner, me_c),
        device_id_type=MESH,
    )
    left_copy.start()
    gate_ref[...] = jax.nn.sigmoid(
        jnp.dot(norm_ref[...], tri_in_ref[4], preferred_element_type=F32)
    )

    def owner_of(slot):
        block_row = slot * 2 + parity
        return block_row // per_col, lax.rem(block_row, per_col)

    def prod_copy(which, d, slot):
        owner, piece = owner_of(slot)
        apart = lax.rem(me_c + nc - owner, nc)
        return pltpu.make_async_remote_copy(
            src_ref=prod_ref.at[which, slot],
            dst_ref=prod_recv.at[me_c, piece],
            send_sem=prod_send_sem.at[which, d],
            recv_sem=prod_recv_sem.at[which, apart * share + piece // 2],
            device_id=(partner if which else me_r, owner),
            device_id_type=MESH,
        )

    def one_block(which, d, slot):
        def step(k, sums):
            right_k = right_all[slot, k].astype(F32)
            return tuple(
                sums[i] + left_ref[which, pl.ds(i * cols + k, 1), :] * right_k
                for i in range(rows)
            )

        sums = lax.fori_loop(
            0, cols, step, tuple(jnp.zeros((rows, chan), F32) for _ in range(rows))
        )
        for i in range(rows):
            prod_ref[which, slot, i] = sums[i].astype(BF16)
        if which:
            prod_copy(which, d, slot).start()
        else:
            owner, piece = owner_of(slot)

            @pl.when(owner != me_c)
            def _():
                prod_copy(which, d, slot).start()

            @pl.when(owner == me_c)
            def _():
                prod_recv[me_c, piece] = prod_ref[which, slot]

    slots = [lax.rem(me_z + line - d, line) for d in range(line)]
    one_block(0, 0, slots[0])
    left_copy.wait()
    left_ref[1] = left_recv[...].astype(F32)
    one_block(1, 0, slots[0])
    for d in range(1, line):
        right_copies[d - 1].wait()
        one_block(1, d, slots[d])
        one_block(0, d, slots[d])
    for e in range(nc):
        source = lax.rem(me_c + e, nc)
        for q in range(share):
            for which in range(2):
                if e or which:
                    piece = 2 * q + (1 - parity if which else parity)
                    pltpu.make_async_remote_copy(
                        src_ref=prod_ref.at[which, 0],
                        dst_ref=prod_recv.at[source, piece],
                        send_sem=prod_send_sem.at[which, 0],
                        recv_sem=prod_recv_sem.at[which, e * share + q],
                        device_id=(partner, me_c),
                        device_id_type=MESH,
                    ).wait_recv()
    for d in range(line):
        prod_copy(1, d, slots[d]).wait_send()
        owner, _ = owner_of(slots[d])

        @pl.when(owner != me_c)
        def _():
            prod_copy(0, d, slots[d]).wait_send()

    for name in ("tri_out", "up", "down"):
        loads[name].wait()
    for i in range(rows):
        for b in range(per_col):
            total = prod_recv[0, b, i].astype(F32)
            for c in range(1, nc):
                total = total + prod_recv[c, b, i].astype(F32)
            start = i * cols + b * rows
            norm_ref[start : start + rows, :] = layer_norm(total).astype(BF16)
    late = mid_ref[...] + gate_ref[...] * jnp.dot(
        norm_ref[...], tri_out_ref[...], preferred_element_type=F32
    )
    normed_late = layer_norm(late).astype(BF16)
    hidden = jnp.maximum(
        jnp.dot(normed_late, up_ref[...], preferred_element_type=F32), 0.0
    ).astype(BF16)
    lowered = jnp.dot(hidden, down_ref[...], preferred_element_type=F32)
    pair_out_ref[...] = (late + lowered).astype(BF16)


def per_device(
    nr,
    nc,
    sequence,
    pair_state,
    residue_mask,
    chain_index,
    attention_in,
    attention_out,
    bias_weight,
    chain_bias,
    outer_in,
    outer_out,
    triangle_in,
    triangle_out,
    transition_up,
    transition_down,
):
    rows, cols, chan = pair_state.shape
    width = sequence.shape[1]
    length = residue_mask.shape[0]
    feats = attention_out.shape[0]
    heads_all = chain_bias.shape[0]
    heads = heads_all // nc
    head_width = feats // heads
    pairs = rows * cols
    per_col = cols // rows
    vmem = pl.BlockSpec(memory_space=pltpu.VMEM)
    sequence_out, pair_out = pl.pallas_call(
        functools.partial(kernel, nr, nc, head_width),
        out_shape=(
            pltpu.VMEM((rows, width), BF16),
            pltpu.VMEM((pairs, chan), BF16),
        ),
        in_specs=[pl.BlockSpec(memory_space=pltpu.HBM)] * 14,
        out_specs=(vmem, vmem),
        scratch_shapes=[
            pltpu.VMEM((nc, heads, pairs), F32),
            pltpu.VMEM((nc, heads, pairs), F32),
            pltpu.VMEM((length, 2 * feats), BF16),
            pltpu.VMEM((rows * heads, length), F32),
            pltpu.VMEM((nc, rows, width), BF16),
            pltpu.VMEM((length, outer_in.shape[1]), BF16),
            pltpu.VMEM((pairs, chan), F32),
            pltpu.VMEM((pairs, chan), BF16),
            pltpu.VMEM((2, pairs, chan), F32),
            pltpu.VMEM((pairs, chan), BF16),
            pltpu.VMEM((pairs, chan), BF16),
            pltpu.VMEM((pairs, chan), F32),
            pltpu.VMEM((pairs, chan), F32),
            pltpu.VMEM((nr // 2, cols, rows, chan), BF16),
            pltpu.VMEM((2, nr // 2, rows, rows, chan), BF16),
            pltpu.VMEM((nc, per_col, rows, rows, chan), BF16),
            pltpu.VMEM((rows, width), BF16),
            pltpu.VMEM((pairs, chan), BF16),
            pltpu.VMEM((1, length), jnp.int32),
            pltpu.VMEM((1, length), jnp.int32),
            pltpu.VMEM(attention_in.shape, BF16),
            pltpu.VMEM(attention_out.shape, BF16),
            pltpu.VMEM((heads_all, chan), BF16),
            pltpu.VMEM((1, heads_all), F32),
            pltpu.VMEM(outer_in.shape, BF16),
            pltpu.VMEM((triangle_in.shape[1], chan, chan), BF16),
            pltpu.VMEM(outer_out.shape, BF16),
            pltpu.VMEM(triangle_out.shape, BF16),
            pltpu.VMEM(transition_up.shape, BF16),
            pltpu.VMEM(transition_down.shape, BF16),
            pltpu.VMEM((rows, 4 * feats), F32),
            pltpu.SemaphoreType.DMA((3, nr)),
            pltpu.SemaphoreType.DMA((3, nr)),
            pltpu.SemaphoreType.DMA((2, nc)),
            pltpu.SemaphoreType.DMA((2, nc)),
            pltpu.SemaphoreType.DMA((2, nr // 2)),
            pltpu.SemaphoreType.DMA((2, nc * (per_col // 2))),
            pltpu.SemaphoreType.DMA((14,)),
        ],
        compiler_params=pltpu.CompilerParams(
            collective_id=0, has_side_effects=True, vmem_limit_bytes=56 * 1024 * 1024
        ),
    )(
        sequence,
        pair_state.reshape(pairs, chan),
        residue_mask.reshape(1, length),
        chain_index.reshape(1, length),
        attention_in,
        attention_out,
        bias_weight.T,
        chain_bias.reshape(1, heads_all),
        outer_in,
        jnp.transpose(triangle_in, (1, 0, 2)),
        outer_out,
        triangle_out,
        transition_up,
        transition_down,
    )
    return sequence_out, pair_out.reshape(rows, cols, chan)


def solution(mesh):
    return jax.shard_map(
        functools.partial(per_device, mesh.shape["row"], mesh.shape["col"]),
        mesh=mesh,
        in_specs=(
            P("row", None),
            P("row", "col", None),
            P(),
            P(),
            P(None, None, "col"),
            P("col", None),
            P(),
            P(),
            P(),
            P(),
            P(),
            P(),
            P(),
            P(),
        ),
        out_specs=(P("row", None), P("row", "col", None)),
        check_vma=False,
    )
```
